32 devices in a mesh: row: 8 (over y, x, core), col: 4 (over z).
Axes of the slice: x: 2, y: 2, z: 4, core: 2. Of those that a mesh axis runs over, the one named last changes fastest.
Arguments:
- position: float32 [3, 131072], P(None, ('row', 'col')), may hold values from -6 to 6
- velocity: float32 [3, 131072], P(None, ('row', 'col')), may hold values from -4 to 4
- accel: float32 [3, 131072], P(None, ('row', 'col')), may hold values from -6 to 6
- jerk: float32 [3, 131072], P(None, ('row', 'col')), may hold values from -6 to 6
- mass: float32 [131072], P(('row', 'col')), may hold values from 3.8146973e-06 to 3.8146973e-05
- elapsed: float32 [131072], P(('row', 'col')), may hold values from 0.01 to 0.1
- active: int32 [2048], P('row'), may hold values from 0 to 131071, as said below
Outputs:
- updated: float32 [12, 2048], P(None, ('row', 'col'))
The draws below stay inside these ranges and needn't reach their ends.
Inputs may be any that keep to these rules, and one draw needn't show every extreme that they name: `active`: distinct body indices; 0 and 131071 always appear.
All inputs are finite; a program needn't handle non-finite values.
Results may differ from the reference program's by a relative error of at most 0.0001.
Values sent between devices are 32-bit elements; how exact they have to be, the bound alone decides.
A program may use at most 64 MiB of HBM per device.

```python
import math
import jax
import jax.numpy as jnp
from jax import lax

NB = 131072
NACT = 2048


def draw_active(key, part):
    first, second = jax.random.split(jax.random.fold_in(key, 7))
    middle = 1 + jax.random.permutation(first, NB - 2)[:NACT - 2]
    listed = jnp.concatenate([jnp.array([0, NB - 1], jnp.int32), middle.astype(jnp.int32)])
    return jax.random.permutation(second, listed).astype(jnp.int32)


def shard_levels(key, extent, cuts, least, largest):
    def one(dim, blocks):
        heights = jax.random.uniform(jax.random.fold_in(jax.random.fold_in(key, 6), dim), (blocks,), jnp.float32, least / len(cuts), largest / len(cuts))
        return jnp.repeat(jnp.exp(heights), extent[dim] // blocks).reshape((-1,) + (1,) * (len(extent) - dim - 1))

    factor_of = one(*cuts[0])
    for cut in cuts[1:]:
        factor_of = factor_of * one(*cut)
    return factor_of


def bell_draw(stream_key, dims, scale, most, pieces=(), dtype=jnp.bfloat16):
    result = scale * jax.random.normal(stream_key, dims, jnp.float32)
    if pieces:
        result = result * shard_levels(stream_key, dims, pieces, -0.22, 0.18)
    return jnp.clip(result, -most, most).astype(dtype)


def setup_inputs(seed: int = 0) -> dict:
    streams_of = jax.random.split(jax.random.key(seed), 8)
    position = bell_draw(streams_of[0], (3, NB), 1.0, 6.0, ((1, 32),), jnp.float32)
    velocity = bell_draw(streams_of[1], (3, NB), 0.5, 4.0, ((1, 32),), jnp.float32)
    accel = bell_draw(streams_of[2], (3, NB), 1.0, 6.0, ((1, 32),), jnp.float32)
    jerk = bell_draw(streams_of[3], (3, NB), 1.0, 6.0, ((1, 32),), jnp.float32)
    mass = jnp.clip(jnp.exp(math.log(3.814697265625e-05) - 2.3025851 * jax.random.uniform(streams_of[4], (NB,), jnp.float32) ** shard_levels(streams_of[4], (NB,), ((0, 32),), -0.2, 0.2)), 3.814697265625e-06, 3.814697265625e-05)
    elapsed = jnp.clip(jnp.exp(math.log(0.1) - 2.3025851 * jax.random.uniform(streams_of[5], (NB,), jnp.float32) ** shard_levels(streams_of[5], (NB,), ((0, 32),), -0.2, 0.2)), 0.01, 0.1)
    active = draw_active(jax.random.fold_in(streams_of[7], 71), 0)
    return dict(position=position, velocity=velocity, accel=accel, jerk=jerk, mass=mass, elapsed=elapsed, active=active)


soft_sq = 0.0025

def predict(raw):
    step = raw[13][None, :]
    pos_new = raw[0:3] + step * raw[3:6] + step * step / 2.0 * raw[6:9] + step * step * step / 6.0 * raw[9:12]
    vel_new = raw[3:6] + step * raw[6:9] + step * step / 2.0 * raw[9:12]
    return (pos_new, vel_new)

def pair_terms(rows_pos, rows_vel, part):
    sep_pos = part[0:3, None, :] - rows_pos[:, :, None]
    sep_vel = part[3:6, None, :] - rows_vel[:, :, None]
    dist_sq = lax.optimization_barrier(jnp.sum(sep_pos * sep_pos, axis=0)) + soft_sq
    inv_dist = lax.rsqrt(dist_sq)
    inv_sq = inv_dist * inv_dist
    mass_term = part[6][None, :] * inv_dist * inv_sq
    radial = 3.0 * lax.optimization_barrier(jnp.sum(sep_pos * sep_vel, axis=0)) * inv_sq
    acc_part = lax.optimization_barrier(jnp.sum(mass_term[None] * sep_pos, axis=2))
    jerk_part = lax.optimization_barrier(jnp.sum(mass_term[None] * (sep_vel - radial[None] * sep_pos), axis=2))
    return jnp.concatenate([acc_part, jerk_part], axis=0)

def interact(rows_pos, rows_vel, cols):
    count = rows_pos.shape[1]
    width = cols.shape[1]
    block = min(width, max(128, 2 ** 21 // count))
    while width % block:
        block = block // 2

    def advance(turn, carry):
        part = lax.dynamic_slice_in_dim(cols, turn * block, block, 1)
        return carry + pair_terms(rows_pos, rows_vel, part)
    return lax.fori_loop(0, width // block, advance, jnp.zeros((6, count), jnp.float32))

def correct(own_raw, forces):
    step = own_raw[13][None, :]
    acc_new = forces[0:3]
    jerk_new = forces[3:6]
    vel_new = own_raw[3:6] + step / 2.0 * (own_raw[6:9] + acc_new) + step * step / 12.0 * (own_raw[9:12] - jerk_new)
    pos_new = own_raw[0:3] + step / 2.0 * (own_raw[3:6] + vel_new) + step * step / 12.0 * (own_raw[6:9] - acc_new)
    return jnp.concatenate([pos_new, vel_new, acc_new, jerk_new], axis=0)

def reference(position, velocity, accel, jerk, mass, elapsed, active):
    raw = jnp.concatenate([position, velocity, accel, jerk, mass[None, :], elapsed[None, :]], axis=0)
    pos_pred, vel_pred = predict(raw)
    cols = jnp.concatenate([pos_pred, vel_pred, mass[None, :]], axis=0)
    rows_raw = jnp.take(raw, active.astype(jnp.int32), axis=1)
    rows_pos, rows_vel = predict(rows_raw)
    forces = interact(rows_pos, rows_vel, cols)
    return correct(rows_raw, forces)
```

```python
import functools

import jax
import jax.numpy as jnp
from jax import lax
from jax.experimental import pallas as pl
from jax.experimental.pallas import tpu as pltpu
from jax.sharding import PartitionSpec as P

soft_sq = 0.0025
f32 = jnp.float32
bf16 = jnp.bfloat16
MESH = pl.DeviceIdType.MESH
WIDE = 128

LEFT = (0, 0, 1, 1, 0, 2)
RIGHT = (0, 1, 0, 1, 2, 0)


def split3(x):
    high = x.astype(bf16).astype(f32)
    rest = x - high
    mid = rest.astype(bf16).astype(f32)
    return high, mid, rest - mid


def take(pieces, order):
    return [pieces[t] for t in order]


def predict(pos, vel, acc, jerk, step):
    pos_new = pos + step * vel + step * step / 2.0 * acc + step * step * step / 6.0 * jerk
    vel_new = vel + step * acc + step * step / 2.0 * jerk
    return pos_new, vel_new


def source_rows(p, q):
    sp, sq = split3(p), split3(q)
    n = split3(jnp.sum(p * p, axis=0, keepdims=True))
    d = split3(jnp.sum(p * q, axis=0, keepdims=True))
    one = jnp.ones_like(n[0])
    return jnp.concatenate(
        take(sp, LEFT) + take(sq, LEFT) + list(n) + list(d) + [one, one, one]
        + [jnp.zeros((WIDE - 45, p.shape[1]), f32)],
        axis=0,
    )


def active_rows(p, q):
    width = p.shape[1]
    sp, sq = split3(p), split3(q)
    n = split3(jnp.sum(p * p, axis=0, keepdims=True) + soft_sq)
    d = split3(jnp.sum(p * q, axis=0, keepdims=True))
    one = jnp.ones_like(n[0])
    z18, z3 = jnp.zeros((18, width), f32), jnp.zeros((3, width), f32)
    tail = jnp.zeros((WIDE - 45, width), f32)
    for_sq = jnp.concatenate(
        [-2.0 * t for t in take(sp, RIGHT)] + [z18, one, one, one, z3] + list(n) + [tail], axis=0
    )
    for_rw = jnp.concatenate(
        [-t for t in take(sq, RIGHT)] + [-t for t in take(sp, RIGHT)] + [z3, one, one, one] + list(d) + [tail],
        axis=0,
    )
    return for_sq.astype(bf16), for_rw.astype(bf16)


def weight_rows(p, q, m):
    return jnp.concatenate(
        list(split3(m * p)) + list(split3(m * q)) + list(split3(m)) + [jnp.zeros((32 - 21, p.shape[1]), f32)],
        axis=0,
    )


def three(a, k):
    return a[k : k + 3] + a[k + 3 : k + 6] + a[k + 6 : k + 9]


def padded(x, rows, lanes):
    if x.shape[0] < rows:
        x = jnp.concatenate([x, jnp.zeros((rows - x.shape[0], x.shape[1]), f32)], axis=0)
    if x.shape[1] < lanes:
        x = jnp.concatenate([x, jnp.zeros((rows, lanes - x.shape[1]), f32)], axis=1)
    return x


def kernel(
    n_row, n_col, share, pos_ref, vel_ref, acc_ref, jerk_ref, mass_ref, step_ref, act_ref, out_ref,
    idx, table, left, weight, mid_ref, give, got, state, f_give, f_got,
    idx_s, idx_r, give_s, give_r, st_s, st_r, f_s, f_r,
):
    n_dev = n_row * n_col
    bodies = pos_ref.shape[1]
    chunks = bodies // WIDE
    act_row = share * n_col
    row, col = lax.axis_index("row"), lax.axis_index("col")
    me = row * n_col + col
    base = me * bodies

    def other(k):
        return lax.rem(me + k, n_dev)

    def at(d):
        return (lax.div(d, n_col), lax.rem(d, n_col))

    def send(src, dst, ss, rs, dev):
        return pltpu.make_async_remote_copy(
            src_ref=src, dst_ref=dst, send_sem=ss, recv_sem=rs, device_id=dev, device_id_type=MESH
        )

    barrier = pltpu.get_barrier_semaphore()

    def greet(k, _):
        pl.semaphore_signal(barrier, inc=1, device_id=at(other(k)), device_id_type=MESH)
        return 0

    lax.fori_loop(1, n_dev, greet, 0)

    for c in range(chunks):
        lane = pl.ds(c * WIDE, WIDE)
        raw = jnp.concatenate(
            [pos_ref[:, lane], vel_ref[:, lane], acc_ref[:, lane], jerk_ref[:, lane], step_ref[:, lane],
             jnp.zeros((3, WIDE), f32)], axis=0,
        )
        for t, piece in enumerate(split3(raw)):
            table[t, pl.ds(c * 16, 16), :] = piece.astype(bf16)

    pl.semaphore_wait(barrier, n_dev - 1)

    def idx_copy(r, slot):
        return send(act_ref, idx.at[slot], idx_s.at[r], idx_r.at[slot], (r, col))

    def idx_start(k, _):
        idx_copy(lax.rem(row + k, n_row), row).start()
        return 0

    lax.fori_loop(1, n_row, idx_start, 0)
    idx[row] = act_ref[...]

    def give_copy(d, slot):
        return send(give.at[d], got.at[slot], give_s.at[d], give_r.at[slot], at(d))

    def pick(k, _):
        r = lax.rem(row + k, n_row)

        @pl.when(k > 0)
        def _():
            idx_copy(r, r).wait_recv()

        offset = idx[r] - base
        high = lax.shift_right_arithmetic(offset, 7)
        low = lax.bitwise_and(offset, 127)
        hot = jnp.where(lax.broadcasted_iota(jnp.int32, (WIDE, act_row), 0) == low, 1.0, 0.0).astype(bf16)
        found = jnp.dot(table[0], hot, preferred_element_type=f32)
        found = found + jnp.dot(table[1], hot, preferred_element_type=f32)
        found = found + jnp.dot(table[2], hot, preferred_element_type=f32)
        mine = jnp.zeros((16, act_row), f32)
        for c in range(chunks):
            mine = mine + jnp.where(high == c, found[c * 16 : (c + 1) * 16], 0.0)
        for c in range(n_col):
            part = mine[:, c * share : (c + 1) * share]
            d = r * n_col + c
            give[d] = padded(jnp.concatenate([part[0:8], part[8:16]], axis=1), 8, WIDE)
        for c in range(n_col):
            d = r * n_col + c

            @pl.when(d != me)
            def _():
                give_copy(d, me).start()

        return 0

    lax.fori_loop(0, n_row, pick, 0)

    p_all, q_all = predict(pos_ref[...], vel_ref[...], acc_ref[...], jerk_ref[...], step_ref[...])
    p_mid = jnp.mean(p_all, axis=1, keepdims=True)
    q_mid = jnp.mean(q_all, axis=1, keepdims=True)
    mid_ref[0:3, :] = jnp.broadcast_to(p_mid, (3, WIDE))
    mid_ref[3:6, :] = jnp.broadcast_to(q_mid, (3, WIDE))
    piece = min(512, bodies)
    for t in range(0, bodies, piece):
        lane = pl.ds(t, piece)
        p, q = predict(pos_ref[:, lane], vel_ref[:, lane], acc_ref[:, lane], jerk_ref[:, lane], step_ref[:, lane])
        p, q = p - p_mid, q - q_mid
        left[lane, :] = source_rows(p, q).T.astype(bf16)
        weight[:, lane] = weight_rows(p, q, mass_ref[:, lane]).astype(bf16)

    def gather(k, total):
        d = other(k)
        give_copy(d, d).wait_recv()
        return total + got[d]

    slab = lax.fori_loop(1, n_dev, gather, give[me])
    x0, v0, a0 = slab[0:3, 0:share], slab[3:6, 0:share], jnp.concatenate(
        [slab[6:8, 0:share], slab[0:1, share : 2 * share]], axis=0)
    j0, step = slab[1:4, share : 2 * share], slab[4:5, share : 2 * share]
    p_own, q_own = predict(x0, v0, a0, j0, step)
    state[me] = padded(jnp.concatenate([p_own, q_own], axis=1), 4, WIDE)

    def state_copy(d, slot):
        return send(state.at[me], state.at[slot], st_s.at[d], st_r.at[slot], at(d))

    def state_start(k, _):
        state_copy(other(k), me).start()
        return 0

    lax.fori_loop(1, n_dev, state_start, 0)

    def f_copy(d, slot):
        return send(f_give.at[d], f_got.at[slot], f_s.at[d], f_r.at[slot], at(d))

    def meet(k, _):
        r = lax.rem(row + k, n_row)
        for c in range(n_col):
            d = r * n_col + c

            @pl.when(d != me)
            def _():
                state_copy(d, d).wait_recv()

        slabs = [state[r * n_col + c] for c in range(n_col)]
        p = jnp.concatenate([s[0:3, 0:share] for s in slabs], axis=1) - mid_ref[0:3, 0:1]
        q = jnp.concatenate([s[0:3, share : 2 * share] for s in slabs], axis=1) - mid_ref[3:6, 0:1]
        for_sq, for_rw = active_rows(p, q)
        b = left[...]
        qt = weight[...]
        dist_sq = jnp.dot(b, for_sq, preferred_element_type=f32)
        r_dot_w = jnp.dot(b, for_rw, preferred_element_type=f32)
        inv = lax.rsqrt(dist_sq)
        inv_sq = inv * inv
        w = inv_sq * inv
        v = (w * inv_sq) * r_dot_w
        wh, vh = w.astype(bf16), v.astype(bf16)
        wl = (w - wh.astype(f32)).astype(bf16)
        vl = (v - vh.astype(f32)).astype(bf16)
        ws = jnp.dot(qt, wh, preferred_element_type=f32) + jnp.dot(qt, wl, preferred_element_type=f32)
        vs = jnp.dot(qt, vh, preferred_element_type=f32) + jnp.dot(qt, vl, preferred_element_type=f32)
        w_sum = ws[18:19] + ws[19:20] + ws[20:21]
        v_sum = vs[18:19] + vs[19:20] + vs[20:21]
        acc = three(ws, 0) - p * w_sum
        jerk = (three(ws, 9) - q * w_sum) - 3.0 * (three(vs, 0) - p * v_sum)
        for c in range(n_col):
            lane = slice(c * share, (c + 1) * share)
            f_give[r * n_col + c] = padded(jnp.concatenate([acc[:, lane], jerk[:, lane]], axis=1), 4, WIDE)
        for c in range(n_col):
            d = r * n_col + c

            @pl.when(d != me)
            def _():
                f_copy(d, me).start()

        return 0

    lax.fori_loop(0, n_row, meet, 0)

    def add_up(k, total):
        d = other(k)
        f_copy(d, d).wait_recv()
        return total + f_got[d]

    forces = lax.fori_loop(1, n_dev, add_up, f_give[me])
    a1, j1 = forces[0:3, 0:share], forces[0:3, share : 2 * share]
    v1 = v0 + step / 2.0 * (a0 + a1) + step * step / 12.0 * (j0 - j1)
    x1 = x0 + step / 2.0 * (v0 + v1) + step * step / 12.0 * (a0 - a1)
    out_ref[...] = jnp.concatenate([x1, v1, a1, j1], axis=0)

    def idx_end(k, _):
        idx_copy(lax.rem(row + k, n_row), row).wait_send()
        return 0

    lax.fori_loop(1, n_row, idx_end, 0)

    def all_end(k, _):
        d = other(k)
        give_copy(d, me).wait_send()
        state_copy(d, me).wait_send()
        f_copy(d, me).wait_send()
        return 0

    lax.fori_loop(1, n_dev, all_end, 0)


def solution(mesh):
    n_row, n_col = mesh.shape["row"], mesh.shape["col"]
    n_dev = n_row * n_col

    def local(position, velocity, accel, jerk, mass, elapsed, active):
        bodies = position.shape[1]
        act_row = active.shape[0]
        share = act_row // n_col
        dma = pltpu.SemaphoreType.DMA
        return pl.pallas_call(
            functools.partial(kernel, n_row, n_col, share),
            out_shape=jax.ShapeDtypeStruct((12, share), f32),
            in_specs=[pl.BlockSpec(memory_space=pltpu.VMEM)] * 7,
            out_specs=pl.BlockSpec(memory_space=pltpu.VMEM),
            scratch_shapes=[
                pltpu.VMEM((n_row, 1, act_row), jnp.int32),
                pltpu.VMEM((3, bodies // WIDE * 16, WIDE), bf16),
                pltpu.VMEM((bodies, WIDE), bf16),
                pltpu.VMEM((32, bodies), bf16),
                pltpu.VMEM((8, WIDE), f32),
                pltpu.VMEM((n_dev, 8, WIDE), f32),
                pltpu.VMEM((n_dev, 8, WIDE), f32),
                pltpu.VMEM((n_dev, 4, WIDE), f32),
                pltpu.VMEM((n_dev, 4, WIDE), f32),
                pltpu.VMEM((n_dev, 4, WIDE), f32),
                dma((n_row,)), dma((n_row,)),
                dma((n_dev,)), dma((n_dev,)),
                dma((n_dev,)), dma((n_dev,)),
                dma((n_dev,)), dma((n_dev,)),
            ],
            compiler_params=pltpu.CompilerParams(
                collective_id=0, has_side_effects=True, vmem_limit_bytes=48 * 2**20
            ),
        )(position, velocity, accel, jerk, mass[None, :], elapsed[None, :], active[None, :])

    both = P(None, ("row", "col"))
    one = P(("row", "col"))
    return jax.shard_map(
        local, mesh=mesh, in_specs=(both, both, both, both, one, one, P("row")), out_specs=both, check_vma=False
    )
```

```python
import functools

import jax
import jax.numpy as jnp
from jax import lax
from jax.experimental import pallas as pl
from jax.experimental.pallas import tpu as pltpu
from jax.sharding import PartitionSpec as P

soft_sq = 0.0025
f32 = jnp.float32
bf16 = jnp.bfloat16
MESH = pl.DeviceIdType.MESH
WIDE = 128

LEFT = (0, 0, 1, 1, 0, 2)
RIGHT = (0, 1, 0, 1, 2, 0)


def split3(x):
    high = x.astype(bf16).astype(f32)
    rest = x - high
    mid = rest.astype(bf16).astype(f32)
    return high, mid, rest - mid


def take(pieces, order):
    return [pieces[t] for t in order]


def predict(pos, vel, acc, jerk, step):
    pos_new = pos + step * vel + step * step / 2.0 * acc + step * step * step / 6.0 * jerk
    vel_new = vel + step * acc + step * step / 2.0 * jerk
    return pos_new, vel_new


def source_rows(p, q):
    sp, sq = split3(p), split3(q)
    n = split3(jnp.sum(p * p, axis=0, keepdims=True))
    d = split3(jnp.sum(p * q, axis=0, keepdims=True))
    one = jnp.ones_like(n[0])
    return jnp.concatenate(
        take(sp, LEFT) + take(sq, LEFT) + list(n) + list(d) + [one, one, one]
        + [jnp.zeros((WIDE - 45, p.shape[1]), f32)],
        axis=0,
    )


def active_rows(p, q):
    width = p.shape[1]
    sp, sq = split3(p), split3(q)
    n = split3(jnp.sum(p * p, axis=0, keepdims=True) + soft_sq)
    d = split3(jnp.sum(p * q, axis=0, keepdims=True))
    one = jnp.ones_like(n[0])
    z18, z3 = jnp.zeros((18, width), f32), jnp.zeros((3, width), f32)
    tail = jnp.zeros((WIDE - 45, width), f32)
    for_sq = jnp.concatenate(
        [-2.0 * t for t in take(sp, RIGHT)] + [z18, one, one, one, z3] + list(n) + [tail], axis=0
    )
    for_rw = jnp.concatenate(
        [-t for t in take(sq, RIGHT)] + [-t for t in take(sp, RIGHT)] + [z3, one, one, one] + list(d) + [tail],
        axis=0,
    )
    return for_sq.astype(bf16), for_rw.astype(bf16)


def weight_rows(p, q, m):
    return jnp.concatenate(
        list(split3(m * p)) + list(split3(m * q)) + list(split3(m)) + [jnp.zeros((32 - 21, p.shape[1]), f32)],
        axis=0,
    )


def three(a, k):
    return a[k : k + 3] + a[k + 3 : k + 6] + a[k + 6 : k + 9]


def padded(x, rows, lanes):
    if x.shape[0] < rows:
        x = jnp.concatenate([x, jnp.zeros((rows - x.shape[0], x.shape[1]), f32)], axis=0)
    if x.shape[1] < lanes:
        x = jnp.concatenate([x, jnp.zeros((rows, lanes - x.shape[1]), f32)], axis=1)
    return x


def kernel(
    n_row, n_col, share, *refs
):
    far, out_ref, near, rest = refs[:7], refs[7], refs[8:15], refs[15:]
    pos_ref, vel_ref, acc_ref, jerk_ref, mass_ref, step_ref, act_ref = near
    (idx, table, left, weight, mid_ref, give, got, row_sum, col_got, own, state, f_give, f_got,
     in_s, idx_s, idx_r, give_s, give_r, col_s, col_r, st_s, st_r, f_s, f_r) = rest
    loads = [pltpu.make_async_copy(a, b, in_s.at[t]) for t, (a, b) in enumerate(zip(far, near))]
    for load in loads:
        load.start()

    n_dev = n_row * n_col
    bodies = pos_ref.shape[1]
    chunks = bodies // WIDE
    act_row = share * n_col
    depth = min(256, bodies)
    row, col = lax.axis_index("row"), lax.axis_index("col")
    me = row * n_col + col
    base = me * bodies

    def other(k):
        return lax.rem(me + k, n_dev)

    def at(d):
        return (lax.div(d, n_col), lax.rem(d, n_col))

    def send(src, dst, ss, rs, dev):
        return pltpu.make_async_remote_copy(
            src_ref=src, dst_ref=dst, send_sem=ss, recv_sem=rs, device_id=dev, device_id_type=MESH
        )

    barrier = pltpu.get_barrier_semaphore()

    def greet(k, _):
        pl.semaphore_signal(barrier, inc=1, device_id=at(other(k)), device_id_type=MESH)
        return 0

    lax.fori_loop(1, n_dev, greet, 0)
    for load in loads:
        load.wait()

    for c in range(chunks):
        lane = pl.ds(c * WIDE, WIDE)
        raw = jnp.concatenate(
            [pos_ref[:, lane], vel_ref[:, lane], acc_ref[:, lane], jerk_ref[:, lane], step_ref[:, lane],
             jnp.zeros((3, WIDE), f32)], axis=0,
        )
        for t, piece in enumerate(split3(raw)):
            table[t, pl.ds(c * 16, 16), :] = piece.astype(bf16)

    pl.semaphore_wait(barrier, n_dev - 1)

    def idx_copy(r, slot):
        return send(act_ref, idx.at[slot], idx_s.at[r], idx_r.at[slot], (r, col))

    def idx_start(k, _):
        idx_copy(lax.rem(row + k, n_row), row).start()
        return 0

    lax.fori_loop(1, n_row, idx_start, 0)
    idx[row] = act_ref[...]

    def give_copy(r, slot):
        return send(give.at[r], got.at[slot], give_s.at[r], give_r.at[slot], (r, col))

    def pick(k, _):
        r = lax.rem(row + k, n_row)

        @pl.when(k > 0)
        def _():
            idx_copy(r, r).wait_recv()

        offset = idx[r] - base
        high = lax.shift_right_arithmetic(offset, 7)
        low = lax.bitwise_and(offset, 127)
        hot = jnp.where(lax.broadcasted_iota(jnp.int32, (WIDE, act_row), 0) == low, 1.0, 0.0).astype(bf16)
        found = jnp.dot(table[0], hot, preferred_element_type=f32)
        found = found + jnp.dot(table[1], hot, preferred_element_type=f32)
        found = found + jnp.dot(table[2], hot, preferred_element_type=f32)
        mine = jnp.zeros((16, act_row), f32)
        for c in range(chunks):
            mine = mine + jnp.where(high == c, found[c * 16 : (c + 1) * 16], 0.0)
        give[r] = mine

        @pl.when(k > 0)
        def _():
            give_copy(r, row).start()

        return 0

    lax.fori_loop(0, n_row, pick, 0)

    p_all, q_all = predict(pos_ref[...], vel_ref[...], acc_ref[...], jerk_ref[...], step_ref[...])
    p_mid = jnp.mean(p_all, axis=1, keepdims=True)
    q_mid = jnp.mean(q_all, axis=1, keepdims=True)
    mid_ref[0:3, :] = jnp.broadcast_to(p_mid, (3, WIDE))
    mid_ref[3:6, :] = jnp.broadcast_to(q_mid, (3, WIDE))
    piece = min(512, bodies)
    for t in range(0, bodies, piece):
        lane = pl.ds(t, piece)
        p, q = predict(pos_ref[:, lane], vel_ref[:, lane], acc_ref[:, lane], jerk_ref[:, lane], step_ref[:, lane])
        p, q = p - p_mid, q - q_mid
        left[lane, :] = source_rows(p, q).T.astype(bf16)
        weight[:, lane] = weight_rows(p, q, mass_ref[:, lane]).astype(bf16)

    def gather(k, total):
        r = lax.rem(row + k, n_row)
        give_copy(r, r).wait_recv()
        return total + got[r]

    row_sum[...] = lax.fori_loop(1, n_row, gather, give[row])

    def col_copy(c, slot):
        return send(row_sum, col_got.at[slot], col_s.at[c], col_r.at[slot], (row, c))

    for k in range(1, n_col):
        col_copy(lax.rem(col + k, n_col), col).start()
    col_got[col] = row_sum[...]
    for k in range(1, n_col):
        c = lax.rem(col + k, n_col)
        col_copy(c, c).wait_recv()
    slab = col_got[0]
    for c in range(1, n_col):
        slab = slab + col_got[c]
    p_row, q_row = predict(slab[0:3], slab[3:6], slab[6:9], slab[9:12], slab[12:13])
    state[row] = padded(jnp.concatenate([p_row, q_row], axis=0), 8, act_row)
    for c in range(n_col):
        own[c] = padded(slab[:, c * share : (c + 1) * share], 16, WIDE)

    def state_copy(r, slot):
        return send(state.at[row], state.at[slot], st_s.at[r], st_r.at[slot], (r, col))

    def state_start(k, _):
        state_copy(lax.rem(row + k, n_row), row).start()
        return 0

    lax.fori_loop(1, n_row, state_start, 0)

    def turn(k):
        if n_row & (n_row - 1):
            return lax.rem(row + k, n_row)
        step_to = jnp.where(k == 0, 0, jnp.where(k == n_row - 1, 1, k + 1))
        return lax.bitwise_xor(row, step_to)

    def f_copy(d, slot):
        return send(f_give.at[d], f_got.at[slot], f_s.at[d], f_r.at[slot], at(d))

    def meet(k, _):
        r = turn(k)

        @pl.when(k > 0)
        def _():
            state_copy(r, r).wait_recv()

        slab = state[r]
        p = slab[0:3] - mid_ref[0:3, 0:1]
        q = slab[3:6] - mid_ref[3:6, 0:1]
        for_sq, for_rw = active_rows(p, q)

        def products(t):
            b = left[pl.ds(t * depth, depth), :]
            return (
                jnp.dot(b, for_sq, preferred_element_type=f32),
                jnp.dot(b, for_rw, preferred_element_type=f32),
            )

        def kernels(dist_sq, r_dot_w):
            inv = lax.rsqrt(dist_sq)
            inv_sq = inv * inv
            w = inv_sq * inv
            v = (w * inv_sq) * r_dot_w
            wh, vh = w.astype(bf16), v.astype(bf16)
            wl = (w - wh.astype(f32)).astype(bf16)
            vl = (v - vh.astype(f32)).astype(bf16)
            return wh, wl, vh, vl

        def sums(total, t, parts):
            qt = weight[:, pl.ds(t * depth, depth)]
            wh, wl, vh, vl = [jnp.dot(qt, x, preferred_element_type=f32) for x in parts]
            return total[0] + (wh + wl), total[1] + (vh + vl)

        blocks = bodies // depth
        zero = jnp.zeros((32, act_row), f32)
        total = (zero, zero)
        now, held = products(0), None
        for t in range(blocks):
            later = products(t + 1) if t + 1 < blocks else None
            parts = kernels(*now)
            if held is not None:
                total = sums(total, t - 1, held)
            now, held = later, parts
        ws, vs = sums(total, blocks - 1, held)
        w_sum = ws[18:19] + ws[19:20] + ws[20:21]
        v_sum = vs[18:19] + vs[19:20] + vs[20:21]
        acc = three(ws, 0) - p * w_sum
        jerk = (three(ws, 9) - q * w_sum) - 3.0 * (three(vs, 0) - p * v_sum)
        for c in range(n_col):
            lane = slice(c * share, (c + 1) * share)
            f_give[r * n_col + c] = padded(jnp.concatenate([acc[:, lane], jerk[:, lane]], axis=1), 4, WIDE)
        for c in range(n_col):
            d = r * n_col + c

            @pl.when(d != me)
            def _():
                f_copy(d, me).start()

        return 0

    lax.fori_loop(0, n_row, meet, 0)

    def add_up(k, total):
        d = other(k)
        f_copy(d, d).wait_recv()
        return total + f_got[d]

    forces = lax.fori_loop(1, n_dev, add_up, f_give[me])
    a1, j1 = forces[0:3, 0:share], forces[0:3, share : 2 * share]
    body = own[col][:, 0:share]
    x0, v0, a0, j0, step = body[0:3], body[3:6], body[6:9], body[9:12], body[12:13]
    v1 = v0 + step / 2.0 * (a0 + a1) + step * step / 12.0 * (j0 - j1)
    x1 = x0 + step / 2.0 * (v0 + v1) + step * step / 12.0 * (a0 - a1)
    out_ref[...] = jnp.concatenate([x1, v1, a1, j1], axis=0)

    def row_end(k, _):
        r = lax.rem(row + k, n_row)
        idx_copy(r, row).wait_send()
        give_copy(r, row).wait_send()
        state_copy(r, row).wait_send()
        return 0

    lax.fori_loop(1, n_row, row_end, 0)
    for k in range(1, n_col):
        col_copy(lax.rem(col + k, n_col), col).wait_send()

    def all_end(k, _):
        f_copy(other(k), me).wait_send()
        return 0

    lax.fori_loop(1, n_dev, all_end, 0)


def solution(mesh):
    n_row, n_col = mesh.shape["row"], mesh.shape["col"]
    n_dev = n_row * n_col

    def local(position, velocity, accel, jerk, mass, elapsed, active):
        bodies = position.shape[1]
        act_row = active.shape[0]
        share = act_row // n_col
        dma = pltpu.SemaphoreType.DMA
        return pl.pallas_call(
            functools.partial(kernel, n_row, n_col, share),
            out_shape=jax.ShapeDtypeStruct((12, share), f32),
            in_specs=[pl.BlockSpec(memory_space=pltpu.MemorySpace.HBM)] * 7,
            out_specs=pl.BlockSpec(memory_space=pltpu.VMEM),
            scratch_shapes=[
                pltpu.VMEM((3, bodies), f32),
                pltpu.VMEM((3, bodies), f32),
                pltpu.VMEM((3, bodies), f32),
                pltpu.VMEM((3, bodies), f32),
                pltpu.VMEM((1, bodies), f32),
                pltpu.VMEM((1, bodies), f32),
                pltpu.VMEM((1, act_row), jnp.int32),
                pltpu.VMEM((n_row, 1, act_row), jnp.int32),
                pltpu.VMEM((3, bodies // WIDE * 16, WIDE), bf16),
                pltpu.VMEM((bodies, WIDE), bf16),
                pltpu.VMEM((32, bodies), bf16),
                pltpu.VMEM((8, WIDE), f32),
                pltpu.VMEM((n_row, 16, act_row), f32),
                pltpu.VMEM((n_row, 16, act_row), f32),
                pltpu.VMEM((16, act_row), f32),
                pltpu.VMEM((n_col, 16, act_row), f32),
                pltpu.VMEM((n_col, 16, WIDE), f32),
                pltpu.VMEM((n_row, 8, act_row), f32),
                pltpu.VMEM((n_dev, 4, WIDE), f32),
                pltpu.VMEM((n_dev, 4, WIDE), f32),
                dma((7,)),
                dma((n_row,)), dma((n_row,)),
                dma((n_row,)), dma((n_row,)),
                dma((n_col,)), dma((n_col,)),
                dma((n_row,)), dma((n_row,)),
                dma((n_dev,)), dma((n_dev,)),
            ],
            compiler_params=pltpu.CompilerParams(
                collective_id=0, has_side_effects=True, vmem_limit_bytes=67043328
            ),
        )(position, velocity, accel, jerk, mass[None, :], elapsed[None, :], active[None, :])

    both = P(None, ("row", "col"))
    one = P(("row", "col"))
    return jax.shard_map(
        local, mesh=mesh, in_specs=(both, both, both, both, one, one, P("row")), out_specs=both, check_vma=False
    )
```

```python
import functools

import jax
import jax.numpy as jnp
from jax import lax
from jax.experimental import pallas as pl
from jax.experimental.pallas import tpu as pltpu
from jax.sharding import PartitionSpec as P

soft_sq = 0.0025
f32 = jnp.float32
bf16 = jnp.bfloat16
MESH = pl.DeviceIdType.MESH
WIDE = 128

LEFT = (0, 0, 1, 1, 0, 2)
RIGHT = (0, 1, 0, 1, 2, 0)


def split3(x):
    high = x.astype(bf16).astype(f32)
    rest = x - high
    mid = rest.astype(bf16).astype(f32)
    return high, mid, rest - mid


def take(pieces, order):
    return [pieces[t] for t in order]


def predict(pos, vel, acc, jerk, step):
    pos_new = pos + step * vel + step * step / 2.0 * acc + step * step * step / 6.0 * jerk
    vel_new = vel + step * acc + step * step / 2.0 * jerk
    return pos_new, vel_new


def source_rows(p, q):
    sp, sq = split3(p), split3(q)
    n = split3(jnp.sum(p * p, axis=0, keepdims=True))
    d = split3(jnp.sum(p * q, axis=0, keepdims=True))
    one = jnp.ones_like(n[0])
    return jnp.concatenate(
        take(sp, LEFT) + take(sq, LEFT) + list(n) + list(d) + [one, one, one]
        + [jnp.zeros((WIDE - 45, p.shape[1]), f32)],
        axis=0,
    )


def active_rows(p, q):
    width = p.shape[1]
    sp, sq = split3(p), split3(q)
    n = split3(jnp.sum(p * p, axis=0, keepdims=True) + soft_sq)
    d = split3(jnp.sum(p * q, axis=0, keepdims=True))
    one = jnp.ones_like(n[0])
    z18, z3 = jnp.zeros((18, width), f32), jnp.zeros((3, width), f32)
    tail = jnp.zeros((WIDE - 45, width), f32)
    for_sq = jnp.concatenate(
        [-2.0 * t for t in take(sp, RIGHT)] + [z18, one, one, one, z3] + list(n) + [tail], axis=0
    )
    for_rw = jnp.concatenate(
        [-t for t in take(sq, RIGHT)] + [-t for t in take(sp, RIGHT)] + [z3, one, one, one] + list(d) + [tail],
        axis=0,
    )
    return for_sq.astype(bf16), for_rw.astype(bf16)


def weight_rows(p, q, m):
    return jnp.concatenate(
        list(split3(m * p)) + list(split3(m * q)) + list(split3(m)) + [jnp.zeros((32 - 21, p.shape[1]), f32)],
        axis=0,
    )


def three(a, k):
    return a[k : k + 3] + a[k + 3 : k + 6] + a[k + 6 : k + 9]


def padded(x, rows, lanes):
    if x.shape[0] < rows:
        x = jnp.concatenate([x, jnp.zeros((rows - x.shape[0], x.shape[1]), f32)], axis=0)
    if x.shape[1] < lanes:
        x = jnp.concatenate([x, jnp.zeros((rows, lanes - x.shape[1]), f32)], axis=1)
    return x


def kernel(
    n_row, n_col, share, *refs
):
    far, out_ref, near, rest = refs[:7], refs[7], refs[8:15], refs[15:]
    pos_ref, vel_ref, acc_ref, jerk_ref, mass_ref, step_ref, act_ref = near
    (idx, table, left, weight, mid_ref, give, got, row_sum, col_got, own, own_got, state, f_give, f_got,
     in_s, idx_s, idx_r, give_s, give_r, col_s, col_r, own_s, own_r, st_s, st_r, f_s, f_r) = rest
    loads = [pltpu.make_async_copy(a, b, in_s.at[t]) for t, (a, b) in enumerate(zip(far, near))]
    for load in loads:
        load.start()

    n_dev = n_row * n_col
    bodies = pos_ref.shape[1]
    chunks = bodies // WIDE
    act_row = share * n_col
    depth = min(256, bodies)
    row, col = lax.axis_index("row"), lax.axis_index("col")
    me = row * n_col + col
    base = me * bodies

    def other(k):
        return lax.rem(me + k, n_dev)

    def at(d):
        return (lax.div(d, n_col), lax.rem(d, n_col))

    def send(src, dst, ss, rs, dev):
        return pltpu.make_async_remote_copy(
            src_ref=src, dst_ref=dst, send_sem=ss, recv_sem=rs, device_id=dev, device_id_type=MESH
        )

    barrier = pltpu.get_barrier_semaphore()

    def greet(k, _):
        pl.semaphore_signal(barrier, inc=1, device_id=(lax.rem(row + k, n_row), col), device_id_type=MESH)
        return 0

    lax.fori_loop(1, n_row, greet, 0)
    for k in range(1, n_col):
        pl.semaphore_signal(barrier, inc=1, device_id=(row, lax.rem(col + k, n_col)), device_id_type=MESH)
    for load in loads:
        load.wait()

    for c in range(chunks):
        lane = pl.ds(c * WIDE, WIDE)
        raw = jnp.concatenate(
            [pos_ref[:, lane], vel_ref[:, lane], acc_ref[:, lane], jerk_ref[:, lane], step_ref[:, lane],
             jnp.zeros((3, WIDE), f32)], axis=0,
        )
        for t, piece in enumerate(split3(raw)):
            table[pl.ds(c * 16, 16), pl.ds(t * WIDE, WIDE)] = piece.astype(bf16)

    pl.semaphore_wait(barrier, n_row - 1 + n_col - 1)

    def idx_copy(r, slot):
        return send(act_ref, idx.at[slot], idx_s.at[r], idx_r.at[slot], (r, col))

    def idx_start(k, _):
        idx_copy(lax.rem(row + k, n_row), row).start()
        return 0

    lax.fori_loop(1, n_row, idx_start, 0)
    idx[row] = act_ref[...]

    def give_copy(r, slot):
        return send(give.at[r], got.at[slot], give_s.at[r], give_r.at[slot], (r, col))

    def pick(k, _):
        r = lax.rem(row + k, n_row)

        @pl.when(k > 0)
        def _():
            idx_copy(r, r).wait_recv()

        offset = idx[r] - base
        high = lax.shift_right_arithmetic(offset, 7)
        low = lax.bitwise_and(offset, 127)
        hot = jnp.where(lax.broadcasted_iota(jnp.int32, (WIDE, act_row), 0) == low, 1.0, 0.0).astype(bf16)
        found = jnp.dot(table[...], jnp.concatenate([hot, hot, hot], axis=0), preferred_element_type=f32)
        mine = jnp.zeros((16, act_row), f32)
        for c in range(chunks):
            mine = mine + jnp.where(high == c, found[c * 16 : (c + 1) * 16], 0.0)
        give[r] = mine

        @pl.when(k > 0)
        def _():
            give_copy(r, row).start()

        return 0

    lax.fori_loop(0, n_row, pick, 0)

    p_all, q_all = predict(pos_ref[...], vel_ref[...], acc_ref[...], jerk_ref[...], step_ref[...])
    p_mid = jnp.mean(p_all, axis=1, keepdims=True)
    q_mid = jnp.mean(q_all, axis=1, keepdims=True)
    mid_ref[0:3, :] = jnp.broadcast_to(p_mid, (3, WIDE))
    mid_ref[3:6, :] = jnp.broadcast_to(q_mid, (3, WIDE))
    piece = min(512, bodies)
    for t in range(0, bodies, piece):
        lane = pl.ds(t, piece)
        p, q = predict(pos_ref[:, lane], vel_ref[:, lane], acc_ref[:, lane], jerk_ref[:, lane], step_ref[:, lane])
        p, q = p - p_mid, q - q_mid
        left[lane, :] = source_rows(p, q).T.astype(bf16)
        weight[:, lane] = weight_rows(p, q, mass_ref[:, lane]).astype(bf16)

    def gather(k, total):
        r = lax.rem(row + k, n_row)
        give_copy(r, r).wait_recv()
        return total + got[r]

    slab = lax.fori_loop(1, n_row, gather, give[row])
    p_row, q_row = predict(slab[0:3], slab[3:6], slab[6:9], slab[9:12], slab[12:13])
    row_sum[...] = padded(jnp.concatenate([p_row, q_row], axis=0), 8, act_row)

    def col_copy(c, slot):
        return send(row_sum, col_got.at[slot], col_s.at[c], col_r.at[slot], (row, c))

    def own_copy(c, slot):
        return send(own.at[c], own_got.at[slot], own_s.at[c], own_r.at[slot], (row, c))

    for k in range(1, n_col):
        col_copy(lax.rem(col + k, n_col), col).start()
    for c in range(n_col):
        own[c] = padded(slab[:, c * share : (c + 1) * share], 16, WIDE)
    col_got[col] = row_sum[...]
    for k in range(1, n_col):
        c = lax.rem(col + k, n_col)
        col_copy(c, c).wait_recv()
    total_state = col_got[0]
    for c in range(1, n_col):
        total_state = total_state + col_got[c]
    state[row] = total_state

    def state_copy(r, slot):
        return send(state.at[row], state.at[slot], st_s.at[r], st_r.at[slot], (r, col))

    def state_start(k, _):
        state_copy(lax.rem(row + k, n_row), row).start()
        return 0

    lax.fori_loop(1, n_row, state_start, 0)
    for k in range(1, n_col):
        own_copy(lax.rem(col + k, n_col), col).start()

    def turn(k):
        if n_row & (n_row - 1):
            return lax.rem(row + k, n_row)
        step_to = jnp.where(k == 0, 0, jnp.where(k == n_row - 1, 1, k + 1))
        return lax.bitwise_xor(row, step_to)

    def f_copy(d, slot):
        return send(f_give.at[d], f_got.at[slot], f_s.at[d], f_r.at[slot], at(d))

    def meet(k, _):
        r = turn(k)

        @pl.when(k > 0)
        def _():
            state_copy(r, r).wait_recv()

        slab = state[r]
        p = slab[0:3] - mid_ref[0:3, 0:1]
        q = slab[3:6] - mid_ref[3:6, 0:1]
        for_sq, for_rw = active_rows(p, q)

        def products(t):
            b = left[pl.ds(t * depth, depth), :]
            return (
                jnp.dot(b, for_sq, preferred_element_type=f32),
                jnp.dot(b, for_rw, preferred_element_type=f32),
            )

        def kernels(dist_sq, r_dot_w):
            inv = lax.rsqrt(dist_sq)
            inv_sq = inv * inv
            w = inv_sq * inv
            v = (w * inv_sq) * r_dot_w
            wh, vh = w.astype(bf16), v.astype(bf16)
            wl = (w - wh.astype(f32)).astype(bf16)
            vl = (v - vh.astype(f32)).astype(bf16)
            return wh, wl, vh, vl

        def sums(total, t, parts):
            qt = weight[:, pl.ds(t * depth, depth)]
            wh, wl, vh, vl = [jnp.dot(qt, x, preferred_element_type=f32) for x in parts]
            return total[0] + (wh + wl), total[1] + (vh + vl)

        blocks = bodies // depth
        zero = jnp.zeros((32, act_row), f32)
        total = (zero, zero)
        now, held = products(0), None
        for t in range(blocks):
            later = products(t + 1) if t + 1 < blocks else None
            parts = kernels(*now)
            if held is not None:
                total = sums(total, t - 1, held)
            now, held = later, parts
        ws, vs = sums(total, blocks - 1, held)
        w_sum = ws[18:19] + ws[19:20] + ws[20:21]
        v_sum = vs[18:19] + vs[19:20] + vs[20:21]
        acc = three(ws, 0) - p * w_sum
        jerk = (three(ws, 9) - q * w_sum) - 3.0 * (three(vs, 0) - p * v_sum)
        for c in range(n_col):
            lane = slice(c * share, (c + 1) * share)
            f_give[r * n_col + c] = padded(jnp.concatenate([acc[:, lane], jerk[:, lane]], axis=1), 4, WIDE)
        for c in range(n_col):
            d = r * n_col + c

            @pl.when(d != me)
            def _():
                f_copy(d, me).start()

        return 0

    lax.fori_loop(0, n_row, meet, 0)

    def add_up(k, total):
        d = other(k)
        f_copy(d, d).wait_recv()
        return total + f_got[d]

    forces = lax.fori_loop(1, n_dev, add_up, f_give[me])
    a1, j1 = forces[0:3, 0:share], forces[0:3, share : 2 * share]
    body = own[col]
    for k in range(1, n_col):
        c = lax.rem(col + k, n_col)
        own_copy(c, c).wait_recv()
        body = body + own_got[c]
    body = body[:, 0:share]
    x0, v0, a0, j0, step = body[0:3], body[3:6], body[6:9], body[9:12], body[12:13]
    v1 = v0 + step / 2.0 * (a0 + a1) + step * step / 12.0 * (j0 - j1)
    x1 = x0 + step / 2.0 * (v0 + v1) + step * step / 12.0 * (a0 - a1)
    out_ref[...] = jnp.concatenate([x1, v1, a1, j1], axis=0)

    def row_end(k, _):
        r = lax.rem(row + k, n_row)
        idx_copy(r, row).wait_send()
        give_copy(r, row).wait_send()
        state_copy(r, row).wait_send()
        return 0

    lax.fori_loop(1, n_row, row_end, 0)
    for k in range(1, n_col):
        c = lax.rem(col + k, n_col)
        col_copy(c, col).wait_send()
        own_copy(c, col).wait_send()

    def all_end(k, _):
        f_copy(other(k), me).wait_send()
        return 0

    lax.fori_loop(1, n_dev, all_end, 0)


def solution(mesh):
    n_row, n_col = mesh.shape["row"], mesh.shape["col"]
    n_dev = n_row * n_col

    def local(position, velocity, accel, jerk, mass, elapsed, active):
        bodies = position.shape[1]
        act_row = active.shape[0]
        share = act_row // n_col
        dma = pltpu.SemaphoreType.DMA
        return pl.pallas_call(
            functools.partial(kernel, n_row, n_col, share),
            out_shape=jax.ShapeDtypeStruct((12, share), f32),
            in_specs=[pl.BlockSpec(memory_space=pltpu.MemorySpace.HBM)] * 7,
            out_specs=pl.BlockSpec(memory_space=pltpu.VMEM),
            scratch_shapes=[
                pltpu.VMEM((3, bodies), f32),
                pltpu.VMEM((3, bodies), f32),
                pltpu.VMEM((3, bodies), f32),
                pltpu.VMEM((3, bodies), f32),
                pltpu.VMEM((1, bodies), f32),
                pltpu.VMEM((1, bodies), f32),
                pltpu.VMEM((1, act_row), jnp.int32),
                pltpu.VMEM((n_row, 1, act_row), jnp.int32),
                pltpu.VMEM((bodies // WIDE * 16, 3 * WIDE), bf16),
                pltpu.VMEM((bodies, WIDE), bf16),
                pltpu.VMEM((32, bodies), bf16),
                pltpu.VMEM((8, WIDE), f32),
                pltpu.VMEM((n_row, 16, act_row), f32),
                pltpu.VMEM((n_row, 16, act_row), f32),
                pltpu.VMEM((8, act_row), f32),
                pltpu.VMEM((n_col, 8, act_row), f32),
                pltpu.VMEM((n_col, 16, WIDE), f32),
                pltpu.VMEM((n_col, 16, WIDE), f32),
                pltpu.VMEM((n_row, 8, act_row), f32),
                pltpu.VMEM((n_dev, 4, WIDE), f32),
                pltpu.VMEM((n_dev, 4, WIDE), f32),
                dma((7,)),
                dma((n_row,)), dma((n_row,)),
                dma((n_row,)), dma((n_row,)),
                dma((n_col,)), dma((n_col,)),
                dma((n_col,)), dma((n_col,)),
                dma((n_row,)), dma((n_row,)),
                dma((n_dev,)), dma((n_dev,)),
            ],
            compiler_params=pltpu.CompilerParams(
                collective_id=0, has_side_effects=True, vmem_limit_bytes=67043328
            ),
        )(position, velocity, accel, jerk, mass[None, :], elapsed[None, :], active[None, :])

    both = P(None, ("row", "col"))
    one = P(("row", "col"))
    return jax.shard_map(
        local, mesh=mesh, in_specs=(both, both, both, both, one, one, P("row")), out_specs=both, check_vma=False
    )
```
